32 devices in a mesh: fsdp: 16 (over z, y, x), tp: 2 (over core).
Axes of the slice: x: 2, y: 2, z: 4, core: 2. Of those that a mesh axis runs over, the one named last changes fastest.
Arguments:
- images: bfloat16 [256, 197, 384], P('fsdp'), may hold values from -6 to 6
- cotangent: bfloat16 [256, 197, 384], P('fsdp'), may hold values from -0.02734375 to 0.02734375
- image_count: int32 [16, 2], P('fsdp'), may hold values from 1 to 8, as said below
- w_qkv: bfloat16 [2, 384, 3, 384], P(None, 'fsdp', None, 'tp'), may hold values from -0.3125 to 0.3125
- w_out: bfloat16 [2, 384, 384], P(None, 'tp', 'fsdp'), may hold values from -1.25 to 1.25
- w_up: bfloat16 [2, 384, 1536], P(None, 'fsdp', 'tp'), may hold values from -0.3125 to 0.3125
- w_down: bfloat16 [2, 1536, 384], P(None, 'tp', 'fsdp'), may hold values from -0.15625 to 0.15625
- vectors: bfloat16 [2, 6, 384], P(None, None, 'fsdp'), may hold values from -2 to 2, as said below
- head_bias: bfloat16 [2, 2, 6, 64], P(None, None, 'tp', 'fsdp'), may hold values from -3 to 3
- up_bias: bfloat16 [2, 24, 64], P(None, 'tp', 'fsdp'), may hold values from -3 to 3
- qkv_moments: float32 [2, 2, 384, 3, 384], P(None, None, 'fsdp', None, 'tp'), may hold values from -0.3 to 0.3, as said below
- out_moments: float32 [2, 2, 384, 384], P(None, None, 'tp', 'fsdp'), may hold values from -0.3 to 0.3, as said below
- up_moments: float32 [2, 2, 384, 1536], P(None, None, 'fsdp', 'tp'), may hold values from -0.3 to 0.3, as said below
- down_moments: float32 [2, 2, 1536, 384], P(None, None, 'tp', 'fsdp'), may hold values from -0.3 to 0.3, as said below
- vector_moments: float32 [2, 2, 6, 384], P(None, None, None, 'fsdp'), may hold values from -0.3 to 0.3, as said below
- head_bias_moments: float32 [2, 2, 2, 6, 64], P(None, None, None, 'tp', 'fsdp'), may hold values from -0.3 to 0.3, as said below
- up_bias_moments: float32 [2, 2, 24, 64], P(None, None, 'tp', 'fsdp'), may hold values from -0.3 to 0.3, as said below
Outputs:
- out_acts: float32 [256, 197, 384], P('fsdp')
- input_grad: float32 [256, 197, 384], P('fsdp')
- grad_qkv: float32 [2, 384, 3, 384], P(None, 'fsdp', None, 'tp')
- grad_out: float32 [2, 384, 384], P(None, 'tp', 'fsdp')
- grad_up: float32 [2, 384, 1536], P(None, 'fsdp', 'tp')
- grad_down: float32 [2, 1536, 384], P(None, 'tp', 'fsdp')
- grad_vectors: float32 [2, 6, 384], P(None, None, 'fsdp')
- grad_head_bias: float32 [2, 2, 6, 64], P(None, None, 'tp', 'fsdp')
- grad_up_bias: float32 [2, 24, 64], P(None, 'tp', 'fsdp')
- new_qkv_moments: float32 [2, 2, 384, 3, 384], P(None, None, 'fsdp', None, 'tp')
- new_out_moments: float32 [2, 2, 384, 384], P(None, None, 'tp', 'fsdp')
- new_up_moments: float32 [2, 2, 384, 1536], P(None, None, 'fsdp', 'tp')
- new_down_moments: float32 [2, 2, 1536, 384], P(None, None, 'tp', 'fsdp')
- new_vector_moments: float32 [2, 2, 6, 384], P(None, None, None, 'fsdp')
- new_head_bias_moments: float32 [2, 2, 2, 6, 64], P(None, None, None, 'tp', 'fsdp')
- new_up_bias_moments: float32 [2, 2, 24, 64], P(None, None, 'tp', 'fsdp')
- update_qkv: float32 [2, 384, 3, 384], P(None, 'fsdp', None, 'tp')
- update_out: float32 [2, 384, 384], P(None, 'tp', 'fsdp')
- update_up: float32 [2, 384, 1536], P(None, 'fsdp', 'tp')
- update_down: float32 [2, 1536, 384], P(None, 'tp', 'fsdp')
- update_vectors: float32 [2, 6, 384], P(None, None, 'fsdp')
- update_head_bias: float32 [2, 2, 6, 64], P(None, None, 'tp', 'fsdp')
- update_up_bias: float32 [2, 24, 64], P(None, 'tp', 'fsdp')
The draws below stay inside these ranges and needn't reach their ends.
Inputs may be any that keep to these rules, and one draw needn't show every extreme that they name: `image_count`: the live images of a group in a micro-batch are its first slots; in every micro-batch some group has all 8 slots live. `vectors`: rows 0 and 3 of each layer hold norm gains, the other rows shifts and biases. `qkv_moments`: index 0 holds first moments, index 1 positive second moments. `out_moments`: index 0 holds first moments, index 1 positive second moments. `up_moments`: index 0 holds first moments, index 1 positive second moments. `down_moments`: index 0 holds first moments, index 1 positive second moments. `vector_moments`: index 0 holds first moments, index 1 positive second moments. `head_bias_moments`: index 0 holds first moments, index 1 positive second moments. `up_bias_moments`: index 0 holds first moments, index 1 positive second moments.
All inputs are finite; a program needn't handle non-finite values.
Results may differ from the reference program's by a relative error of at most 0.024.
Values may be sent and summed in bfloat16 or wider, within the bound.
No kernel may reach another device: no remote copies, remote signals or barrier semaphores. Data moves between devices by JAX's collectives and lax.ppermute only.
A program may use at most 256 MiB of HBM per device.

```python
import math
import jax
import jax.numpy as jnp
from jax import lax

D = 384
H = 6
HD = 64
FF = 1536
SEQ = 197
LAYERS = 2
MICRO = 2
IMG_MB = 8
ADAM_STEP = 4
IMG_DEV = 16
GROUPS = 16
IMAGES = 256


def moment_pair(key, shape, label):
    key_own = jax.random.fold_in(key, label)
    key_first, key_second = jax.random.split(key_own)
    first_moment = 0.05 * jnp.clip(jax.random.normal(key_first, shape, jnp.float32), -6.0, 6.0)
    second_moment = 0.005 * jnp.exp(jax.random.uniform(key_second, shape, jnp.float32, 0.0, math.log(10.0)))
    return jnp.stack([first_moment, second_moment])


def draw_image_count(key, part):
    key_base, key_full = jax.random.split(key)
    counts_drawn = jax.random.randint(key_base, (GROUPS, MICRO), 1, IMG_MB + 1)
    full_group = jax.random.randint(key_full, (MICRO,), 0, GROUPS)
    is_full = jnp.arange(GROUPS)[:, None] == full_group[None, :]
    return jnp.where(is_full, IMG_MB, counts_drawn).astype(jnp.int32)


def draw_vectors(key, part):
    noise_draw = jnp.clip(jax.random.normal(key, (LAYERS, 6, D), jnp.float32), -4.0, 4.0)
    is_gain = (jnp.arange(6) % 3 == 0)[None, :, None]
    return jnp.where(is_gain, 1.0 + 0.15 * noise_draw, 0.5 * noise_draw).astype(jnp.bfloat16)


def draw_qkv_moments(key, part):
    return moment_pair(key, (LAYERS, D, 3, H * HD), 101)


def draw_out_moments(key, part):
    return moment_pair(key, (LAYERS, H * HD, D), 102)


def draw_up_moments(key, part):
    return moment_pair(key, (LAYERS, D, FF), 103)


def draw_down_moments(key, part):
    return moment_pair(key, (LAYERS, FF, D), 104)


def draw_vector_moments(key, part):
    return moment_pair(key, (LAYERS, 6, D), 105)


def draw_head_bias_moments(key, part):
    return moment_pair(key, (LAYERS, 2, H, HD), 106)


def draw_up_bias_moments(key, part):
    return moment_pair(key, (LAYERS, FF // HD, HD), 107)


def block_scale(own_key, dims, shards, low, largest):
    level, own = 1.0, jax.random.fold_in(own_key, 6)
    for position, blocks in shards:
        draws = jnp.exp(jax.random.uniform(jax.random.fold_in(own, position), (blocks,), jnp.float32, low / len(shards), largest / len(shards)))
        level = level * jnp.repeat(draws, dims[position] // blocks).reshape([-1 if axis == position else 1 for axis in range(len(dims))])
    return level


def gaussian(rng, shape, spread, bound, shards=(), held_as=jnp.bfloat16):
    loudness = block_scale(rng, shape, shards, -0.22, 0.18) if shards else 1.0
    array = jax.random.normal(rng, shape, jnp.float32) * spread * loudness
    return jnp.minimum(jnp.maximum(array, -bound), bound).astype(held_as)


def setup_inputs(seed: int = 0) -> dict:
    seeds = jax.random.split(jax.random.key(seed), 18)
    return {
        "images": gaussian(seeds[0], (IMAGES, SEQ, D), 1.0, 6.0, ((0, 16),)),
        "cotangent": gaussian(seeds[1], (IMAGES, SEQ, D), ((IMAGES * SEQ) ** (0 - 0.5)), 0.02734375, ((0, 16),)),
        "image_count": draw_image_count(jax.random.fold_in(seeds[17], 71), 0),
        "w_qkv": gaussian(seeds[3], (LAYERS, D, 3, H * HD), D ** -0.5, 0.3125, ((1, 16), (3, 2))),
        "w_out": gaussian(seeds[4], (LAYERS, H * HD, D), (H * HD // 16) ** -0.5, 1.25, ((1, 2), (2, 16))),
        "w_up": gaussian(seeds[5], (LAYERS, D, FF), D ** -0.5, 0.3125, ((1, 16), (2, 2))),
        "w_down": gaussian(seeds[6], (LAYERS, FF, D), FF ** -0.5, 0.15625, ((1, 2), (2, 16))),
        "vectors": draw_vectors(jax.random.fold_in(seeds[17], 71), 0),
        "head_bias": gaussian(seeds[8], (LAYERS, 2, H, HD), 0.5, 3.0, ((2, 2), (3, 16))),
        "up_bias": gaussian(seeds[9], (LAYERS, FF // HD, HD), 0.5, 3.0, ((1, 2), (2, 16))),
        "qkv_moments": draw_qkv_moments(jax.random.fold_in(seeds[17], 71), 0),
        "out_moments": draw_out_moments(jax.random.fold_in(seeds[17], 71), 0),
        "up_moments": draw_up_moments(jax.random.fold_in(seeds[17], 71), 0),
        "down_moments": draw_down_moments(jax.random.fold_in(seeds[17], 71), 0),
        "vector_moments": draw_vector_moments(jax.random.fold_in(seeds[17], 71), 0),
        "head_bias_moments": draw_head_bias_moments(jax.random.fold_in(seeds[17], 71), 0),
        "up_bias_moments": draw_up_bias_moments(jax.random.fold_in(seeds[17], 71), 0),
    }


EPS_NORM = 1e-06
LEARN_RATE = 0.05
BETA_ONE = 0.9
BETA_TWO = 0.95
ADAM_EPS = 1e-08
DECAY_RATE = 0.05
HIGH = lax.Precision.HIGHEST

@jax.custom_vjp
def low(v):
    return lax.optimization_barrier(v.astype(jnp.bfloat16)).astype(jnp.float32)

@jax.custom_vjp
def low_back(v):
    return v

def low_keep(v):
    return (low(v), None)

def low_pass(kept, grad):
    return (grad,)

def back_keep(v):
    return (v, None)

def back_low(kept, grad):
    return (low(grad),)
low.defvjp(low_keep, low_pass)
low_back.defvjp(back_keep, back_low)

def norm_apply(values, gain_row, shift_row):
    centre = values - lax.optimization_barrier(jnp.mean(values, axis=-1, keepdims=True))
    variance = lax.optimization_barrier(jnp.mean(centre * centre, axis=-1, keepdims=True))
    return centre * lax.rsqrt(variance + EPS_NORM) * gain_row + shift_row

def block_forward(stream, qkv_weight, out_weight, up_weight, down_weight, vector_rows, head_biases, up_biases):
    batch_size = stream.shape[0]
    seq_len = stream.shape[1]
    normed = low(norm_apply(stream, vector_rows[0], vector_rows[1]))
    mixed_proj = jnp.einsum('bsd,dkc->bskc', normed, qkv_weight, precision=HIGH)
    query = low(low_back(mixed_proj[:, :, 0] + head_biases[0].reshape(-1)))
    keys_all = low(low_back(mixed_proj[:, :, 1]))
    values_all = low(low_back(mixed_proj[:, :, 2] + head_biases[1].reshape(-1)))
    head_shape = (batch_size, seq_len, H, HD)
    scores = low_back(jnp.einsum('bqhe,bkhe->bhqk', query.reshape(head_shape), keys_all.reshape(head_shape), precision=HIGH) * 0.125)
    probs_low = low(jax.nn.softmax(scores, axis=-1))
    attended = jnp.einsum('bhqk,bkhe->bqhe', probs_low, values_all.reshape(head_shape), precision=HIGH)
    attended = low(low_back(attended.reshape(batch_size, seq_len, H * HD)))
    branch = low_back(jnp.einsum('bsc,cd->bsd', attended, out_weight, precision=HIGH))
    middle = stream + branch + vector_rows[2]
    normed_two = low(norm_apply(middle, vector_rows[3], vector_rows[4]))
    hidden = low_back(jnp.einsum('bsd,df->bsf', normed_two, up_weight, precision=HIGH) + up_biases.reshape(-1))
    activated = low(jax.nn.gelu(hidden, approximate=False))
    branch_two = low_back(jnp.einsum('bsf,fd->bsd', activated, down_weight, precision=HIGH))
    return middle + branch_two + vector_rows[5]

def whole_forward(stream, params):
    for layer_idx in range(LAYERS):
        stream = block_forward(stream, *[member[layer_idx] for member in params])
    return stream

def adam_step(weight_now, gradient, moments):
    first_moment = BETA_ONE * moments[0] + (1.0 - BETA_ONE) * gradient
    second_moment = BETA_TWO * moments[1] + (1.0 - BETA_TWO) * gradient * gradient
    first_fix = first_moment / (1.0 - BETA_ONE ** ADAM_STEP)
    second_fix = second_moment / (1.0 - BETA_TWO ** ADAM_STEP)
    change = -LEARN_RATE * (first_fix / (jnp.sqrt(second_fix) + ADAM_EPS) + DECAY_RATE * weight_now)
    return (jnp.stack([first_moment, second_moment]), change)

def reference(images, cotangent, image_count, w_qkv, w_out, w_up, w_down, vectors, head_bias, up_bias, qkv_moments, out_moments, up_moments, down_moments, vector_moments, head_bias_moments, up_bias_moments):
    params = tuple((member.astype(jnp.float32) for member in (w_qkv, w_out, w_up, w_down, vectors, head_bias, up_bias)))
    slot_index = jnp.arange(IMAGES, dtype=jnp.int32)
    group_of = slot_index // IMG_DEV
    micro_of = slot_index % IMG_DEV // IMG_MB
    live_mask = (slot_index % IMG_MB < image_count[group_of, micro_of]).astype(jnp.float32)
    per_groups = 1
    target_groups = max(1, 4096 // (IMG_DEV * SEQ))
    while per_groups * 2 <= target_groups and GROUPS % (per_groups * 2) == 0:
        per_groups = per_groups * 2
    block_images = per_groups * IMG_DEV
    block_count = IMAGES // block_images
    inputs_blocks = images.astype(jnp.float32).reshape(block_count, block_images, SEQ, D)
    cot_blocks = cotangent.astype(jnp.float32).reshape(block_count, block_images, SEQ, D)
    mask_blocks = live_mask.reshape(block_count, block_images)

    def step_block(totals, block_in):
        inputs_here, cot_here, mask_here = block_in

        def masked(stream, weights):
            return whole_forward(stream, weights) * mask_here[:, None, None]
        outputs_here, pullback = jax.vjp(masked, inputs_here, params)
        grad_inputs, grad_params = pullback(cot_here)
        totals = jax.tree.map(lambda left, right: left + right, totals, grad_params)
        return (totals, (outputs_here, grad_inputs))
    zero_totals = tuple((jnp.zeros(member.shape, jnp.float32) for member in params))
    grad_totals, (outputs_all, grads_all) = lax.scan(step_block, zero_totals, (inputs_blocks, cot_blocks, mask_blocks))
    out_acts = outputs_all.reshape(IMAGES, SEQ, D)
    input_grad = grads_all.reshape(IMAGES, SEQ, D)
    moment_list = (qkv_moments, out_moments, up_moments, down_moments, vector_moments, head_bias_moments, up_bias_moments)
    new_moments = []
    updates = []
    for index_p in range(7):
        moved, change = adam_step(params[index_p], grad_totals[index_p], moment_list[index_p])
        new_moments.append(moved)
        updates.append(change)
    return (out_acts, input_grad, grad_totals[0], grad_totals[1], grad_totals[2], grad_totals[3], grad_totals[4], grad_totals[5], grad_totals[6], new_moments[0], new_moments[1], new_moments[2], new_moments[3], new_moments[4], new_moments[5], new_moments[6], updates[0], updates[1], updates[2], updates[3], updates[4], updates[5], updates[6])
```

```python
from functools import partial

import jax
import jax.numpy as jnp
from jax import lax
from jax.sharding import PartitionSpec as P

D = 384
HD = 64
SEQ = 197
LAYERS = 2
MICRO = 2
IMG_MB = 8
ADAM_STEP = 4
IMG_DEV = 16


EPS_NORM = 1e-06
LEARN_RATE = 0.05
BETA_ONE = 0.9
BETA_TWO = 0.95
ADAM_EPS = 1e-08
DECAY_RATE = 0.05


def norm_parts(values, gain_row, shift_row):
    centre = values - jnp.mean(values, axis=-1, keepdims=True)
    variance = jnp.mean(centre * centre, axis=-1, keepdims=True)
    inverse = lax.rsqrt(variance + EPS_NORM)
    scaled = centre * inverse
    return (scaled * gain_row + shift_row, scaled, inverse)


def norm_back(grad_normed, scaled, inverse, gain_row):
    grad_scaled = grad_normed * gain_row
    return inverse * (
        grad_scaled
        - jnp.mean(grad_scaled, axis=-1, keepdims=True)
        - scaled * jnp.mean(grad_scaled * scaled, axis=-1, keepdims=True)
    )


def token_sum(values):
    return jnp.sum(values, axis=(0, 1))


def layer_forward(stream, weights, reducers):
    qkv_weight, out_weight, up_weight, down_weight, vector_rows, head_biases, up_biases = weights
    vec_rows = vector_rows.astype(jnp.float32)
    batch_size, seq_len, width = stream.shape
    heads_here = head_biases.shape[1]
    normed, scaled_one, inverse_one = norm_parts(stream, vec_rows[0], vec_rows[1])
    normed_low = normed.astype(jnp.bfloat16)
    mixed_proj = jnp.einsum(
        "bsd,dkc->bskc", normed_low, qkv_weight, preferred_element_type=jnp.float32
    )
    bias_rows = head_biases.astype(jnp.float32).reshape(2, -1)
    query_low = (mixed_proj[:, :, 0] + bias_rows[0]).astype(jnp.bfloat16)
    keys_low = mixed_proj[:, :, 1].astype(jnp.bfloat16)
    values_low = (mixed_proj[:, :, 2] + bias_rows[1]).astype(jnp.bfloat16)
    head_shape = (batch_size, seq_len, heads_here, HD)
    scores = (
        jnp.einsum(
            "bqhe,bkhe->bhqk",
            query_low.reshape(head_shape),
            keys_low.reshape(head_shape),
            preferred_element_type=jnp.float32,
        )
        * 0.125
    )
    log_total = jax.nn.logsumexp(scores, axis=-1, keepdims=True)
    probs_low = jnp.exp(scores - log_total).astype(jnp.bfloat16)
    attended = jnp.einsum(
        "bhqk,bkhe->bqhe",
        probs_low,
        values_low.reshape(head_shape),
        preferred_element_type=jnp.float32,
    )
    attended_low = attended.reshape(batch_size, seq_len, heads_here * HD).astype(jnp.bfloat16)
    branch = jnp.einsum("bsc,cd->bsd", attended_low, out_weight, preferred_element_type=jnp.float32)
    branch = reducers[0](branch)
    middle = stream + branch + vec_rows[2]
    normed_two, scaled_two, inverse_two = norm_parts(middle, vec_rows[3], vec_rows[4])
    normed_two_low = normed_two.astype(jnp.bfloat16)
    hidden = jnp.einsum(
        "bsd,df->bsf", normed_two_low, up_weight, preferred_element_type=jnp.float32
    )
    hidden = hidden + up_biases.astype(jnp.float32).reshape(-1)
    activated_low = jax.nn.gelu(hidden, approximate=False).astype(jnp.bfloat16)
    branch_two = jnp.einsum(
        "bsf,fd->bsd", activated_low, down_weight, preferred_element_type=jnp.float32
    )
    branch_two = reducers[1](branch_two)
    result = middle + branch_two + vec_rows[5]
    cache = (
        scaled_one,
        inverse_one,
        normed_low,
        query_low,
        keys_low,
        values_low,
        log_total,
        attended_low,
        scaled_two,
        inverse_two,
        normed_two_low,
        hidden,
    )
    return (result, cache)


def layer_backward(grad_stream, weights, cache, reducers):
    qkv_weight, out_weight, up_weight, down_weight, vector_rows, head_biases, up_biases = weights
    (
        scaled_one,
        inverse_one,
        normed_low,
        query_low,
        keys_low,
        values_low,
        log_total,
        attended_low,
        scaled_two,
        inverse_two,
        normed_two_low,
        hidden,
    ) = cache
    vec_rows = vector_rows.astype(jnp.float32)
    batch_size, seq_len, width = grad_stream.shape
    heads_here = head_biases.shape[1]
    head_shape = (batch_size, seq_len, heads_here, HD)
    grad_mlp_bias = token_sum(grad_stream)
    grad_stream_low = grad_stream.astype(jnp.bfloat16)
    activated, gelu_back = jax.vjp(partial(jax.nn.gelu, approximate=False), hidden)
    activated_low = activated.astype(jnp.bfloat16)
    grad_down_w = jnp.einsum(
        "bsf,bsd->fd", activated_low, grad_stream_low, preferred_element_type=jnp.float32
    )
    grad_act = jnp.einsum(
        "bsd,fd->bsf", grad_stream_low, down_weight, preferred_element_type=jnp.float32
    )
    grad_hidden_low = gelu_back(grad_act)[0].astype(jnp.bfloat16)
    grad_up_b = token_sum(grad_hidden_low.astype(jnp.float32)).reshape(up_biases.shape)
    grad_up_w = jnp.einsum(
        "bsd,bsf->df", normed_two_low, grad_hidden_low, preferred_element_type=jnp.float32
    )
    grad_normed_two = jnp.einsum(
        "bsf,df->bsd", grad_hidden_low, up_weight, preferred_element_type=jnp.float32
    )
    grad_normed_two = reducers[2](grad_normed_two)
    grad_gain_two = token_sum(grad_normed_two * scaled_two)
    grad_shift_two = token_sum(grad_normed_two)
    grad_middle = grad_stream + norm_back(grad_normed_two, scaled_two, inverse_two, vec_rows[3])
    grad_out_bias = token_sum(grad_middle)
    grad_middle_low = grad_middle.astype(jnp.bfloat16)
    grad_out_w = jnp.einsum(
        "bsc,bsd->cd", attended_low, grad_middle_low, preferred_element_type=jnp.float32
    )
    grad_att_low = (
        jnp.einsum("bsd,cd->bsc", grad_middle_low, out_weight, preferred_element_type=jnp.float32)
        .astype(jnp.bfloat16)
        .reshape(head_shape)
    )
    query_heads = query_low.reshape(head_shape)
    keys_heads = keys_low.reshape(head_shape)
    values_heads = values_low.reshape(head_shape)
    scores = (
        jnp.einsum("bqhe,bkhe->bhqk", query_heads, keys_heads, preferred_element_type=jnp.float32)
        * 0.125
    )
    probs = jnp.exp(scores - log_total)
    probs_low = probs.astype(jnp.bfloat16)
    grad_probs = jnp.einsum(
        "bqhe,bkhe->bhqk", grad_att_low, values_heads, preferred_element_type=jnp.float32
    )
    grad_values = jnp.einsum(
        "bhqk,bqhe->bkhe", probs_low, grad_att_low, preferred_element_type=jnp.float32
    )
    grad_scores_low = (
        probs * (grad_probs - jnp.sum(grad_probs * probs, axis=-1, keepdims=True))
    ).astype(jnp.bfloat16)
    grad_query = (
        jnp.einsum(
            "bhqk,bkhe->bqhe", grad_scores_low, keys_heads, preferred_element_type=jnp.float32
        )
        * 0.125
    )
    grad_keys = (
        jnp.einsum(
            "bhqk,bqhe->bkhe", grad_scores_low, query_heads, preferred_element_type=jnp.float32
        )
        * 0.125
    )
    flat_shape = (batch_size, seq_len, heads_here * HD)
    grad_mixed_low = jnp.stack(
        [
            grad_query.reshape(flat_shape),
            grad_keys.reshape(flat_shape),
            grad_values.reshape(flat_shape),
        ],
        axis=2,
    ).astype(jnp.bfloat16)
    grad_head_b = jnp.stack(
        [
            token_sum(grad_mixed_low[:, :, 0].astype(jnp.float32)),
            token_sum(grad_mixed_low[:, :, 2].astype(jnp.float32)),
        ]
    ).reshape(head_biases.shape)
    grad_qkv_w = jnp.einsum(
        "bsd,bskc->dkc", normed_low, grad_mixed_low, preferred_element_type=jnp.float32
    )
    grad_normed = jnp.einsum(
        "bskc,dkc->bsd", grad_mixed_low, qkv_weight, preferred_element_type=jnp.float32
    )
    grad_normed = reducers[3](grad_normed)
    grad_gain_one = token_sum(grad_normed * scaled_one)
    grad_shift_one = token_sum(grad_normed)
    grad_input = grad_middle + norm_back(grad_normed, scaled_one, inverse_one, vec_rows[0])
    grad_vec = jnp.stack(
        [grad_gain_one, grad_shift_one, grad_out_bias, grad_gain_two, grad_shift_two, grad_mlp_bias]
    )
    return (
        grad_input,
        (grad_qkv_w, grad_out_w, grad_up_w, grad_down_w, grad_vec, grad_head_b, grad_up_b),
    )


def adam_step(weight_now, gradient, moments):
    first_moment = BETA_ONE * moments[0] + (1.0 - BETA_ONE) * gradient
    second_moment = BETA_TWO * moments[1] + (1.0 - BETA_TWO) * gradient * gradient
    first_fix = first_moment / (1.0 - BETA_ONE**ADAM_STEP)
    second_fix = second_moment / (1.0 - BETA_TWO**ADAM_STEP)
    change = -LEARN_RATE * (
        first_fix / (jnp.sqrt(second_fix) + ADAM_EPS) + DECAY_RATE * weight_now.astype(jnp.float32)
    )
    return (jnp.stack([first_moment, second_moment]), change)


def radix_bits(count):
    bits = []
    while (1 << len(bits)) < count:
        bits.append(1 << len(bits))
    return bits


def swap_with(values, bit, axis, size):
    return lax.ppermute(values, axis, [(dev, dev ^ bit) for dev in range(size)])


def gather_order(size, swap_tail):
    bits = radix_bits(size)
    tail = bits[:2]
    if swap_tail:
        tail = tail[::-1]
    return bits[2:] + tail


def gather_rows(shard, size, swap_tail):
    index = lax.axis_index("fsdp")
    done = []
    block = shard[None]
    for bit in gather_order(size, swap_tail):
        other = swap_with(block, bit, "fsdp", size)
        high = (index & bit) != 0
        first = jnp.where(high, other, block)
        second = jnp.where(high, block, other)
        done.append(bit)
        done.sort(reverse=True)
        place = done.index(bit)
        lead = 1 << place
        rest = block.shape[0] // lead
        shape = (lead, rest) + shard.shape
        block = jnp.stack([first.reshape(shape), second.reshape(shape)], axis=1)
        block = block.reshape((lead * 2 * rest,) + shard.shape)
    return block


def scatter_rows(full, size, swap_tail):
    index = lax.axis_index("fsdp")
    left = sorted(radix_bits(size), reverse=True)
    block = full
    for bit in gather_order(size, swap_tail)[::-1]:
        place = left.index(bit)
        lead = 1 << place
        rest = block.shape[0] // lead // 2
        split = block.reshape((lead, 2, rest) + full.shape[1:])
        high = (index & bit) != 0
        keep = jnp.where(high, split[:, 1], split[:, 0])
        send = jnp.where(high, split[:, 0], split[:, 1]).astype(jnp.bfloat16)
        got = swap_with(send, bit, "fsdp", size)
        block = (keep + got.astype(jnp.float32)).reshape((lead * rest,) + full.shape[1:])
        left.remove(bit)
    return block[0]


def swap_cores(values):
    return lax.ppermute(values, "tp", [(0, 1), (1, 0)])


def pack_small(vectors, head_bias, up_bias):
    rows = up_bias.shape[0] * up_bias.shape[1]
    vec = vectors.reshape(-1, vectors.shape[-1])
    hb = head_bias.reshape(-1, head_bias.shape[-1])
    ub = up_bias.reshape(-1, up_bias.shape[-1])
    vec = jnp.pad(vec, ((0, rows - vec.shape[0]), (0, 0)))
    hb = jnp.pad(hb, ((0, rows - hb.shape[0]), (0, 0)))
    small = jnp.concatenate([vec, hb, ub], axis=1)
    return jnp.pad(small, ((0, 0), (0, 128 - small.shape[1])))


def per_device(
    sizes,
    images,
    cotangent,
    image_count,
    w_qkv,
    w_out,
    w_up,
    w_down,
    vectors,
    head_bias,
    up_bias,
    qkv_moments,
    out_moments,
    up_moments,
    down_moments,
    vector_moments,
    head_bias_moments,
    up_bias_moments,
):
    fsdp = sizes
    core = lax.axis_index("tp")
    rows = w_qkv.shape[1]
    heads_here = head_bias.shape[2]
    groups_here = up_bias.shape[1]
    cols = w_qkv.shape[3]
    hidden = w_up.shape[2]
    dv, dh, du = vectors.shape[2], head_bias.shape[3], up_bias.shape[2]

    small = gather_rows(pack_small(vectors, head_bias, up_bias), fsdp, False)
    small_two = swap_cores(small)

    def vec_of(block):
        return block[:, :12, :dv].transpose(1, 0, 2).reshape(LAYERS, 6, D)

    def hb_of(block):
        part = block[:, : 4 * heads_here, dv : dv + dh]
        return part.transpose(1, 0, 2).reshape(LAYERS, 2, heads_here, HD)

    def ub_of(block):
        part = block[:, :, dv + dh : dv + dh + du]
        return part.transpose(1, 0, 2).reshape(LAYERS, groups_here, HD)

    vec_full = vec_of(small)
    hb_full = jnp.concatenate([hb_of(small), hb_of(small_two)], axis=2)
    ub_full = jnp.concatenate([ub_of(small), ub_of(small_two)], axis=1)

    layer_weights = []
    for l in range(LAYERS):
        attn = jnp.concatenate([w_qkv[l].reshape(rows, 3 * cols), w_out[l].T], axis=1)
        halves = []
        for part, tail in ((attn, False), (w_up[l], True), (w_down[l].T, False)):
            own = gather_rows(part, fsdp, tail).reshape(D, -1)
            halves.append((own, swap_cores(own)))
        attn_h, up_h, down_h = halves
        q_full = jnp.concatenate([h[:, : 3 * cols].reshape(D, 3, cols) for h in attn_h], axis=2)
        o_full = jnp.concatenate([h[:, 3 * cols :] for h in attn_h], axis=1).T
        u_full = jnp.concatenate(up_h, axis=1)
        d_full = jnp.concatenate(down_h, axis=1).T
        layer_weights.append((q_full, o_full, u_full, d_full, vec_full[l], hb_full[l], ub_full[l]))

    reducers = (lambda v: v,) * 4
    first = core * IMG_MB
    live = (jnp.arange(IMG_MB, dtype=jnp.int32) < image_count[0, core]).astype(jnp.float32)
    live_mask = live[:, None, None]
    stream = lax.dynamic_slice_in_dim(images, first, IMG_MB, 0).astype(jnp.float32)
    caches = []
    for l in range(LAYERS):
        stream, cache = layer_forward(stream, layer_weights[l], reducers)
        caches.append(cache)
    out_own = stream * live_mask
    grad_stream = (
        lax.dynamic_slice_in_dim(cotangent, first, IMG_MB, 0).astype(jnp.float32) * live_mask
    )
    owned_layers = [None] * LAYERS
    small_grads = [None] * LAYERS
    for l in reversed(range(LAYERS)):
        grad_stream, grads = layer_backward(grad_stream, layer_weights[l], caches[l], reducers)
        gq, go, gu, gd, gv, gh, gb = grads
        own_other = []
        for h in range(2):
            c = slice(h * cols, (h + 1) * cols)
            f = slice(h * hidden, (h + 1) * hidden)
            own_other.append(
                (
                    jnp.concatenate([gq[:, :, c].reshape(D, 3 * cols), go[c].T], axis=1),
                    gu[:, f],
                    gd[f].T,
                )
            )
        owned = []
        for own, other, tail in zip(own_other[0], own_other[1], (False, True, False)):
            got = swap_cores(other.astype(jnp.bfloat16)).astype(jnp.float32)
            summed = (own + got).reshape(fsdp, rows, -1)
            owned.append(scatter_rows(summed, fsdp, tail))
        owned_layers[l] = owned
        small_grads[l] = (gv, gh, gb)
    gv = jnp.stack([small_grads[l][0] for l in range(LAYERS)])
    gh = jnp.stack([small_grads[l][1] for l in range(LAYERS)])
    gb = jnp.stack([small_grads[l][2] for l in range(LAYERS)])

    def small_pack(h):
        hsl = slice(h * heads_here, (h + 1) * heads_here)
        gsl = slice(h * groups_here, (h + 1) * groups_here)
        nrow = LAYERS * groups_here
        a = gv.reshape(12, fsdp, dv).transpose(1, 0, 2)
        b = gh[:, :, hsl].reshape(4 * heads_here, fsdp, dh).transpose(1, 0, 2)
        c = gb[:, gsl].reshape(nrow, fsdp, du).transpose(1, 0, 2)
        a = jnp.pad(a, ((0, 0), (0, nrow - a.shape[1]), (0, 0)))
        b = jnp.pad(b, ((0, 0), (0, nrow - b.shape[1]), (0, 0)))
        packed = jnp.concatenate([a, b, c], axis=2)
        return jnp.pad(packed, ((0, 0), (0, 0), (0, 128 - packed.shape[2])))

    small_sum = scatter_rows(small_pack(0) + swap_cores(small_pack(1)), fsdp, False)
    g_vec = small_sum[:12, :dv].reshape(LAYERS, 6, dv)
    g_hb = small_sum[: 4 * heads_here, dv : dv + dh].reshape(LAYERS, 2, heads_here, dh)
    g_ub = small_sum[:, dv + dh : dv + dh + du].reshape(LAYERS, groups_here, du)
    owned = (
        jnp.stack([o[0][:, : 3 * cols].reshape(rows, 3, cols) for o in owned_layers]),
        jnp.stack([o[0][:, 3 * cols :].T for o in owned_layers]),
        jnp.stack([o[1] for o in owned_layers]),
        jnp.stack([o[2].T for o in owned_layers]),
        g_vec,
        g_hb,
        g_ub,
    )

    def both(own):
        other = swap_cores(own)
        low = core == 0
        return jnp.concatenate([jnp.where(low, own, other), jnp.where(low, other, own)])

    out_acts = both(out_own)
    input_grad = both(grad_stream)
    param_list = (w_qkv, w_out, w_up, w_down, vectors, head_bias, up_bias)
    moment_list = (
        qkv_moments,
        out_moments,
        up_moments,
        down_moments,
        vector_moments,
        head_bias_moments,
        up_bias_moments,
    )
    new_moments = []
    updates = []
    for index_p in range(7):
        moved, change = adam_step(param_list[index_p], owned[index_p], moment_list[index_p])
        new_moments.append(moved)
        updates.append(change)
    return (out_acts, input_grad, *owned, *new_moments, *updates)


def solution(mesh):
    placed = (
        P("fsdp", None, None),
        P("fsdp", None, None),
        P("fsdp", None),
        P(None, "fsdp", None, "tp"),
        P(None, "tp", "fsdp"),
        P(None, "fsdp", "tp"),
        P(None, "tp", "fsdp"),
        P(None, None, "fsdp"),
        P(None, None, "tp", "fsdp"),
        P(None, "tp", "fsdp"),
        P(None, None, "fsdp", None, "tp"),
        P(None, None, "tp", "fsdp"),
        P(None, None, "fsdp", "tp"),
        P(None, None, "tp", "fsdp"),
        P(None, None, None, "fsdp"),
        P(None, None, None, "tp", "fsdp"),
        P(None, None, "tp", "fsdp"),
    )
    return jax.shard_map(
        partial(per_device, mesh.shape["fsdp"]),
        mesh=mesh,
        in_specs=placed,
        out_specs=(
            P("fsdp", None, None),
            P("fsdp", None, None),
            P(None, "fsdp", None, "tp"),
            P(None, "tp", "fsdp"),
            P(None, "fsdp", "tp"),
            P(None, "tp", "fsdp"),
            P(None, None, "fsdp"),
            P(None, None, "tp", "fsdp"),
            P(None, "tp", "fsdp"),
            P(None, None, "fsdp", None, "tp"),
            P(None, None, "tp", "fsdp"),
            P(None, None, "fsdp", "tp"),
            P(None, None, "tp", "fsdp"),
            P(None, None, None, "fsdp"),
            P(None, None, None, "tp", "fsdp"),
            P(None, None, "tp", "fsdp"),
            P(None, "fsdp", None, "tp"),
            P(None, "tp", "fsdp"),
            P(None, "fsdp", "tp"),
            P(None, "tp", "fsdp"),
            P(None, None, "fsdp"),
            P(None, None, "tp", "fsdp"),
            P(None, "tp", "fsdp"),
        ),
        check_vma=False,
    )
```

```python
from functools import partial

import jax
import jax.numpy as jnp
from jax import lax
from jax.experimental import pallas as pl
from jax.experimental.pallas import tpu as pltpu
from jax.sharding import PartitionSpec as P

D = 384
HD = 64
HEADS = 6
FF = 1536
SEQ = 197
PAD = 208
LAYERS = 2
IMG_MB = 8
STEP_IMG = 2
ROWS = STEP_IMG * PAD
STEPS = IMG_MB // STEP_IMG
ADAM_STEP = 4

EPS_NORM = 1e-06
LEARN_RATE = 0.05
BETA_ONE = 0.9
BETA_TWO = 0.95
ADAM_EPS = 1e-08
DECAY_RATE = 0.05

F32 = jnp.float32
BF16 = jnp.bfloat16
LOW = -1e30

INV_SQRT_2PI = 0.3989422804014327
INV_SQRT_2 = 0.7071067811865476
LOG2_E = 1.4426950408889634
CHUNK = 256


def dot_nn(a, b):
    return lax.dot_general(a, b, (((1,), (0,)), ((), ())), preferred_element_type=F32)


def dot_nt(a, b):
    return lax.dot_general(a, b, (((1,), (1,)), ((), ())), preferred_element_type=F32)


def dot_tn(a, b):
    return lax.dot_general(a, b, (((0,), (0,)), ((), ())), preferred_element_type=F32)


def row_loop(chunk, body, carry=None, total=ROWS):
    for i in range(total // chunk):
        carry = body(slice(i * chunk, (i + 1) * chunk), carry)
    return carry


def norm_stats(x):
    centre = x - jnp.mean(x, axis=-1, keepdims=True)
    inverse = lax.rsqrt(jnp.mean(centre * centre, axis=-1, keepdims=True) + EPS_NORM)
    return centre * inverse, inverse


def norm_to(x_ref, gain, shift, dst):
    def body(rows, c):
        scaled, _ = norm_stats(x_ref[rows, :])
        dst[rows, :] = (scaled * gain + shift).astype(BF16)
        return c

    row_loop(32, body, 0)


def norm_back_rows(x, e, gain):
    scaled, inverse = norm_stats(x)
    eg = e * gain
    back = inverse * (
        eg
        - jnp.mean(eg, axis=-1, keepdims=True)
        - scaled * jnp.mean(eg * scaled, axis=-1, keepdims=True)
    )
    return back, scaled


def fold8(v):
    return v[0:8] + v[8:16] + v[16:24] + v[24:32]


def total8(v):
    return jnp.sum(v, axis=0, keepdims=True)


def zeros8(n):
    return jnp.zeros((8, n), F32)


def gelu_pair(u):
    cdf = 0.5 * lax.erf(u * INV_SQRT_2) + 0.5
    tail = jnp.exp2(u * u * (-0.5 * LOG2_E))
    return u * cdf, cdf + (u * INV_SQRT_2PI) * tail


def head_masks():
    lane = lax.broadcasted_iota(jnp.int32, (1, 2 * HD), 1)
    first = (lane < HD).astype(F32)
    second = 1.0 - first
    return first.astype(BF16), second.astype(BF16)


def load_attn_weights(own, oth, wqkv, wout):
    q = D // 2
    for j in range(3):
        wqkv[:, j * D : (j + 1) * D] = jnp.concatenate(
            [own[:, j * q : (j + 1) * q], oth[:, j * q : (j + 1) * q]], axis=1
        )
    wout[...] = jnp.concatenate([own[:, 3 * q :], oth[:, 3 * q :]], axis=1)


def attn_forward(x, small, wqkv, wout, a, qkv, probs, att, st, mid):
    norm_to(x, small[0:1, :], small[1:2, :], a)
    for j in range(3):
        part = dot_nn(a[...], wqkv[:, j * D : (j + 1) * D])
        if j == 0:
            part = part + small[6:7, :]
        elif j == 2:
            part = part + small[7:8, :]
        qkv[:, j * D : (j + 1) * D] = part.astype(BF16)
    masks = head_masks()
    cut = PAD - 16

    def image(im, c):
        rows = pl.ds(pl.multiple_of(im * PAD, 16), PAD)
        keep = lax.broadcasted_iota(jnp.int32, (16, PAD), 0) < SEQ - cut

        def part(which, head):
            lo = which * D + head // 2 * 128
            return qkv[rows, lo : lo + 128]

        def score(head):
            mask = (masks[head % 2] * 0.125).astype(BF16)
            st[head % 2] = dot_nt(part(1, head), part(0, head) * mask)

        score(0)
        both = None
        for head in range(HEADS):
            if head + 1 < HEADS:
                score(head + 1)
            slot = st.at[head % 2]
            top = slot[:cut]
            end = jnp.where(keep, slot[cut:], LOW)
            peak = jnp.maximum(
                jnp.max(top, axis=0, keepdims=True), jnp.max(end, axis=0, keepdims=True)
            )
            top = jnp.exp(top - peak)
            end = jnp.exp(end - peak)
            total = jnp.sum(top, axis=0, keepdims=True) + jnp.sum(end, axis=0, keepdims=True)
            scale = 1.0 / total
            low = jnp.concatenate([(top * scale).astype(BF16), (end * scale).astype(BF16)], axis=0)
            probs[im * HEADS + head] = low
            out = dot_tn(part(2, head) * masks[head % 2], low)
            both = out if head % 2 == 0 else both + out
            if head % 2:
                att[rows, (head // 2) * 128 : (head // 2 + 1) * 128] = both.T.astype(BF16)
        return c

    lax.fori_loop(0, STEP_IMG, image, 0)
    mid[...] = x[...] + dot_nt(att[...], wout[...]) + small[2:3, :]


def mlp_forward(mid, small, ub, ups, downs, b, z, gp, out):
    norm_to(mid, small[3:4, :], small[4:5, :], b)
    half = FF // 2
    for lo in range(0, FF, CHUNK):
        cols = slice(lo, lo + CHUNK)
        src = ups[lo // half]
        u = dot_nn(b[...], src[:, lo % half : lo % half + CHUNK]) + ub[0:1, cols]
        act, slope = gelu_pair(u)
        z[:, cols] = act.astype(BF16)
        gp[:, cols] = slope.astype(BF16)
    out[...] = (
        mid[...]
        + dot_nt(z[:, :half], downs[0][...])
        + dot_nt(z[:, half:], downs[1][...])
        + small[5:6, :]
    )


def mlp_backward(g, mid, small, ups, downs, z, gp, b, gb, du, d_up, d_down, d_small, d_ub, dm):
    def low(rows, c):
        v = g[rows, :]
        gb[rows, :] = v.astype(BF16)
        return c + fold8(v)

    d_small[5:6, :] += total8(row_loop(32, low, zeros8(D)))
    d_down[...] += dot_tn(gb[...], z[...])
    half = FF // 2
    for lo in range(0, FF, CHUNK):
        cols = slice(lo, lo + CHUNK)
        src = downs[lo // half]
        dz = dot_nn(gb[...], src[:, lo % half : lo % half + CHUNK])
        v = (dz * gp[:, cols].astype(F32)).astype(BF16)
        du[:, cols] = v
        d_ub[0:1, cols] += jnp.sum(v.astype(F32), axis=0, keepdims=True)
    norm_to(mid, small[3:4, :], small[4:5, :], b)
    d_up[...] += dot_tn(b[...], du[...])
    dm[...] = dot_nt(du[:, :half], ups[0][...]) + dot_nt(du[:, half:], ups[1][...])
    gain = small[3:4, :]

    def back(rows, c):
        e = dm[rows, :]
        grad, scaled = norm_back_rows(mid[rows, :], e, gain)
        v = g[rows, :] + grad
        dm[rows, :] = v
        return c[0] + fold8(e * scaled), c[1] + fold8(e), c[2] + fold8(v)

    sums = row_loop(32, back, (zeros8(D),) * 3)
    d_small[3:4, :] += total8(sums[0])
    d_small[4:5, :] += total8(sums[1])
    d_small[2:3, :] += total8(sums[2])


def attn_backward(dm, x, small, wqkv, wout, qkv, probs, att, a, gb, do, dqkv, st, d_attn, d_small, dx):
    def low(rows, c):
        gb[rows, :] = dm[rows, :].astype(BF16)
        return c

    row_loop(32, low, 0)
    d_attn[:, 3 * D :] += dot_tn(gb[...], att[...])
    do[...] = dot_nn(gb[...], wout[...]).astype(BF16)
    masks = head_masks()

    def image(im, c):
        rows = pl.ds(pl.multiple_of(im * PAD, 16), PAD)

        def part(which, head):
            lo = which * D + head // 2 * 128
            return qkv[rows, lo : lo + 128]

        def dout(head):
            lo = head // 2 * 128
            return do[rows, lo : lo + 128] * masks[head % 2]

        def score(head):
            st[head % 2] = dot_nt(part(2, head), dout(head))

        score(0)
        kept = None
        for head in range(HEADS):
            if head + 1 < HEADS:
                score(head + 1)
            pr = probs[im * HEADS + head]
            prf = pr.astype(F32)
            dp = st[head % 2]
            mean = jnp.sum(dp * prf, axis=0, keepdims=True)
            ds = (prf * (dp - mean)).astype(BF16)
            eighth = (masks[head % 2] * 0.125).astype(BF16)
            new = (
                dot_tn(part(1, head) * eighth, ds),
                dot_nn(ds, part(0, head) * eighth),
                dot_nn(pr, dout(head)),
            )
            kept = new if head % 2 == 0 else tuple(p + q for p, q in zip(kept, new))
            if head % 2:
                lo = head // 2 * 128
                dqkv[rows, lo : lo + 128] = kept[0].T.astype(BF16)
                dqkv[rows, D + lo : D + lo + 128] = kept[1].astype(BF16)
                dqkv[rows, 2 * D + lo : 2 * D + lo + 128] = kept[2].astype(BF16)
        return c

    lax.fori_loop(0, STEP_IMG, image, 0)

    def bias(rows, c):
        return (
            c[0] + fold8(dqkv[rows, 0:D].astype(F32)),
            c[1] + fold8(dqkv[rows, 2 * D : 3 * D].astype(F32)),
        )

    sums = row_loop(32, bias, (zeros8(D),) * 2)
    d_small[6:7, :] += total8(sums[0])
    d_small[7:8, :] += total8(sums[1])
    norm_to(x, small[0:1, :], small[1:2, :], a)
    d_attn[:, : 3 * D] += dot_tn(a[...], dqkv[...])
    dx[...] = dot_nt(dqkv[...], wqkv[...])
    gain = small[0:1, :]

    def back(rows, c):
        e = dx[rows, :]
        grad, scaled = norm_back_rows(x[rows, :], e, gain)
        dx[rows, :] = dm[rows, :] + grad
        return c[0] + fold8(e * scaled), c[1] + fold8(e)

    sums = row_loop(32, back, (zeros8(D),) * 2)
    d_small[0:1, :] += total8(sums[0])
    d_small[1:2, :] += total8(sums[1])


def first_step(body):
    pl.when(pl.program_id(0) == 0)(body)


def last_step(body):
    pl.when(pl.program_id(0) == STEPS - 1)(body)


def store_attn_grads(d_attn, own, oth):
    q = D // 2
    for dst, lo in ((own, 0), (oth, q)):
        dst[...] = jnp.concatenate(
            [d_attn[:, j * D + lo : j * D + lo + q] for j in range(4)], axis=1
        ).astype(BF16)


def store_mlp_grads(d_mat, own, oth):
    half = FF // 2
    own[...] = d_mat[:, :half].astype(BF16)
    oth[...] = d_mat[:, half:].astype(BF16)


def load_images(src, dst):
    for im in range(STEP_IMG):
        dst[im * PAD : im * PAD + SEQ, :] = src[im].astype(F32)


def kernel_attn0(core, img, own, oth, small, mid, qkv, probs, att, x, wqkv, wout, a, st):
    @first_step
    def _():
        x[...] = jnp.zeros_like(x)
        load_attn_weights(own, oth, wqkv, wout)

    load_images(img, x)
    attn_forward(x, small, wqkv, wout, a, qkv, probs, att, st, mid)


def kernel_mlp0(mid, up_a, up_b, dn_a, dn_b, small, ub, out, z, gp, b):
    mlp_forward(mid, small, ub, (up_a, up_b), (dn_a, dn_b), b, z, gp, out)


def kernel_layer1(
    core, count, x, cot, own, oth, up_a, up_b, dn_a, dn_b, small, ub,
    acts, dx, g_own, g_oth, g_up_own, g_up_oth, g_dn_own, g_dn_oth, g_small, g_ub,
    wqkv, wout, a, st, qkv, probs, att, mid, b, z, gp, y, g, gb, du, do, dqkv, dm,
    d_attn, d_up, d_down, d_small, d_ub,
):
    @first_step
    def _():
        load_attn_weights(own, oth, wqkv, wout)
        g[...] = jnp.zeros_like(g)
        for ref in (d_attn, d_up, d_down, d_small, d_ub):
            ref[...] = jnp.zeros_like(ref)

    ups, downs = (up_a, up_b), (dn_a, dn_b)
    attn_forward(x, small, wqkv, wout, a, qkv, probs, att, st, mid)
    mlp_forward(mid, small, ub, ups, downs, b, z, gp, y)
    for im in range(STEP_IMG):
        slot = pl.program_id(0) * STEP_IMG + im
        live = (slot < count[0]).astype(F32)
        acts[im] = y[im * PAD : im * PAD + SEQ, :] * live
        g[im * PAD : im * PAD + SEQ, :] = cot[im].astype(F32) * live
    mlp_backward(g, mid, small, ups, downs, z, gp, b, gb, du, d_up, d_down, d_small, d_ub, dm)
    attn_backward(dm, x, small, wqkv, wout, qkv, probs, att, a, gb, do, dqkv, st, d_attn, d_small, dx)

    @last_step
    def _():
        store_attn_grads(d_attn, g_own, g_oth)
        store_mlp_grads(d_up, g_up_own, g_up_oth)
        store_mlp_grads(d_down, g_dn_own, g_dn_oth)
        g_small[...] = d_small[...]
        g_ub[...] = d_ub[...]


def kernel_mlp0_back(
    g, mid, z, gp, up_a, up_b, dn_a, dn_b, small,
    dm, g_up_own, g_up_oth, g_dn_own, g_dn_oth, g_small, g_ub,
    b, gb, du, d_up, d_down, d_small, d_ub,
):
    @first_step
    def _():
        for ref in (d_up, d_down, d_small, d_ub):
            ref[...] = jnp.zeros_like(ref)

    mlp_backward(
        g, mid, small, (up_a, up_b), (dn_a, dn_b), z, gp, b, gb, du, d_up, d_down, d_small, d_ub, dm
    )

    @last_step
    def _():
        store_mlp_grads(d_up, g_up_own, g_up_oth)
        store_mlp_grads(d_down, g_dn_own, g_dn_oth)
        g_small[...] = d_small[...]
        g_ub[...] = d_ub[...]


def kernel_attn0_back(
    core, img, dm, qkv, probs, att, own, oth, small,
    dx, g_own, g_oth, g_small,
    x, wqkv, wout, a, gb, do, dqkv, st, dxs, d_attn, d_small,
):
    @first_step
    def _():
        x[...] = jnp.zeros_like(x)
        load_attn_weights(own, oth, wqkv, wout)
        for ref in (d_attn, d_small):
            ref[...] = jnp.zeros_like(ref)

    load_images(img, x)
    attn_backward(dm, x, small, wqkv, wout, qkv, probs, att, a, gb, do, dqkv, st, d_attn, d_small, dxs)
    for im in range(STEP_IMG):
        dx[im] = dxs[im * PAD : im * PAD + SEQ, :]

    @last_step
    def _():
        store_attn_grads(d_attn, g_own, g_oth)
        g_small[...] = d_small[...]


def tokens(width):
    return pl.BlockSpec((ROWS, width), lambda i, *s: (i, 0))


def whole(*shape):
    return pl.BlockSpec(shape, lambda i, *s: (0,) * len(shape))


def my_images():
    return pl.BlockSpec((STEP_IMG, SEQ, D), lambda i, core, *s: (core[0] * STEPS + i, 0, 0))


def step_images():
    return pl.BlockSpec((STEP_IMG, SEQ, D), lambda i, *s: (i, 0, 0))


def prob_spec():
    return pl.BlockSpec((STEP_IMG * HEADS, PAD, PAD), lambda i, *s: (i, 0, 0))


def shape(*dims, dtype=F32):
    return jax.ShapeDtypeStruct(dims, dtype)


TOK = IMG_MB * PAD
HALF = 2 * D


def call(kernel, prefetch, in_specs, out_specs, out_shape, scratch, name, gflop):
    return pl.pallas_call(
        kernel,
        grid_spec=pltpu.PrefetchScalarGridSpec(
            num_scalar_prefetch=prefetch,
            grid=(STEPS,),
            in_specs=in_specs,
            out_specs=out_specs,
            scratch_shapes=[pltpu.VMEM(s, d) for s, d in scratch],
        ),
        out_shape=out_shape,
        name=name,
        cost_estimate=pl.CostEstimate(
            flops=int(gflop * 1e9), transcendentals=0, bytes_accessed=16 * 1024 * 1024
        ),
        compiler_params=pltpu.CompilerParams(
            dimension_semantics=("arbitrary",), vmem_limit_bytes=60 * 1024 * 1024
        ),
    )


W_SPEC = lambda: whole(D, HALF)
QKV_S = ((D, 3 * D), BF16)
WO_S = ((D, D), BF16)
ROW_B = ((ROWS, D), BF16)
ROW_F = ((ROWS, D), F32)
ST_S = ((2, PAD, PAD), F32)
ROW_3B = ((ROWS, 3 * D), BF16)
ROW_FB = ((ROWS, FF), BF16)
PROB_S = ((STEP_IMG * HEADS, PAD, PAD), BF16)


def run_attn0(core, images, own, oth, small):
    return call(
        kernel_attn0, 1,
        [my_images(), W_SPEC(), W_SPEC(), whole(8, D)],
        [tokens(D), tokens(3 * D), prob_spec(), tokens(D)],
        [shape(TOK, D), shape(TOK, 3 * D, dtype=BF16), shape(IMG_MB * HEADS, PAD, PAD, dtype=BF16), shape(TOK, D, dtype=BF16)],
        [ROW_F, QKV_S, WO_S, ROW_B, ST_S], "attn0", 10,
    )(core, images, own, oth, small)


def run_mlp0(mid, ups, downs, small, ub):
    return call(
        kernel_mlp0, 0,
        [tokens(D)] + [W_SPEC() for _ in range(4)] + [whole(8, D), whole(1, FF)],
        [tokens(D), tokens(FF), tokens(FF)],
        [shape(TOK, D), shape(TOK, FF, dtype=BF16), shape(TOK, FF, dtype=BF16)],
        [ROW_B], "mlp0", 16,
    )(mid, *ups, *downs, small, ub)


def run_layer1(core, count, x, cot, attn, ups, downs, small, ub):
    gshape = shape(D, HALF, dtype=BF16)
    return call(
        kernel_layer1, 2,
        [tokens(D), my_images()] + [W_SPEC() for _ in range(6)] + [whole(8, D), whole(1, FF)],
        [step_images(), tokens(D)] + [W_SPEC() for _ in range(6)] + [whole(8, D), whole(1, FF)],
        [shape(IMG_MB, SEQ, D), shape(TOK, D)] + [gshape] * 6 + [shape(8, D), shape(1, FF)],
        [QKV_S, WO_S, ROW_B, ST_S, ROW_3B, PROB_S, ROW_B, ROW_F, ROW_B, ROW_FB, ROW_FB, ROW_F, ROW_F,
         ROW_B, ROW_FB, ROW_B, ROW_3B, ROW_F,
         ((D, 4 * D), F32), ((D, FF), F32), ((D, FF), F32), ((8, D), F32), ((1, FF), F32)], "layer1", 60,
    )(core, count, x, cot, *attn, *ups, *downs, small, ub)


def run_mlp0_back(g, mid, z, gp, ups, downs, small):
    gshape = shape(D, HALF, dtype=BF16)
    return call(
        kernel_mlp0_back, 0,
        [tokens(D), tokens(D), tokens(FF), tokens(FF)] + [W_SPEC() for _ in range(4)] + [whole(8, D)],
        [tokens(D)] + [W_SPEC() for _ in range(4)] + [whole(8, D), whole(1, FF)],
        [shape(TOK, D)] + [gshape] * 4 + [shape(8, D), shape(1, FF)],
        [ROW_B, ROW_B, ROW_FB, ((D, FF), F32), ((D, FF), F32), ((8, D), F32), ((1, FF), F32)], "mlp0_back", 20,
    )(g, mid, z, gp, *ups, *downs, small)


def run_attn0_back(core, images, dm, qkv, probs, att, own, oth, small):
    gshape = shape(D, HALF, dtype=BF16)
    return call(
        kernel_attn0_back, 1,
        [my_images(), tokens(D), tokens(3 * D), prob_spec(), tokens(D), W_SPEC(), W_SPEC(), whole(8, D)],
        [step_images(), W_SPEC(), W_SPEC(), whole(8, D)],
        [shape(IMG_MB, SEQ, D), gshape, gshape, shape(8, D)],
        [ROW_F, QKV_S, WO_S, ROW_B, ROW_B, ROW_B, ROW_3B, ST_S, ROW_F, ((D, 4 * D), F32), ((8, D), F32)], "attn0_back", 20,
    )(core, images, dm, qkv, probs, att, own, oth, small)


def high_bits(size):
    return [1 << k for k in range(2, size.bit_length() - 1)]


def swap_bit(values, bit, size):
    return lax.ppermute(values, "fsdp", [(dev, dev ^ bit) for dev in range(size)])


def swap_split(values, bits, size):
    pairs = [(2 * dev + c, 2 * (dev ^ bits[c]) + c) for dev in range(size) for c in range(2)]
    return lax.ppermute(values, ("fsdp", "tp"), pairs)


def swap_cores(values):
    return lax.ppermute(values, "tp", [(0, 1), (1, 0)])


def gather_rows(shard, size):
    index = lax.axis_index("fsdp")
    zero_core = lax.axis_index("tp") == 0
    block = shard[None]
    for bit in high_bits(size):
        other = swap_bit(block, bit, size)
        high = (index & bit) != 0
        block = jnp.concatenate([jnp.where(high, other, block), jnp.where(high, block, other)])
    low = (index & 1) != 0
    mid = (index & 2) != 0
    one = jnp.where(zero_core, low, mid)
    two = jnp.where(zero_core, mid, low)
    other = swap_split(block, (1, 2), size)
    pair = jnp.stack([jnp.where(one, other, block), jnp.where(one, block, other)])
    got = swap_split(pair, (2, 1), size)
    near = jnp.where(two, pair[1], got[1])
    far = jnp.where(two, got[1], pair[1])
    near0 = jnp.where(two, pair[0], got[0])
    far0 = jnp.where(two, got[0], pair[0])
    quad = [far0, jnp.where(zero_core, far, near0), jnp.where(zero_core, near0, far), near]
    full = jnp.stack(quad, axis=1)
    return full.reshape((size,) + shard.shape)


def scatter_rows(full, size):
    index = lax.axis_index("fsdp")
    core = lax.axis_index("tp")
    low = index & 1
    mid = (index >> 1) & 1
    one = jnp.where(core == 0, low, mid)
    two = jnp.where(core == 0, mid, low)
    quad = full.reshape((size // 4, 4) + full.shape[1:])

    def pick(which, j):
        return lax.dynamic_index_in_dim(
            quad, jnp.where(core == 0, which * 2 + j, j * 2 + which), 1, keepdims=False
        )

    send = jnp.stack([pick(1 - two, 0), pick(1 - two, 1)]).astype(BF16)
    got = swap_split(send, (2, 1), size)
    block = jnp.stack([pick(two, 0), pick(two, 1)]).astype(F32) + got.astype(F32)
    send = lax.dynamic_index_in_dim(block, 1 - one, 0, keepdims=False).astype(BF16)
    got = swap_split(send, (1, 2), size)
    block = lax.dynamic_index_in_dim(block, one, 0, keepdims=False) + got.astype(F32)
    for bit in high_bits(size)[::-1]:
        split = block.reshape((2, block.shape[0] // 2) + block.shape[1:])
        which = jnp.where((index & bit) != 0, 1, 0)
        send = lax.dynamic_index_in_dim(split, 1 - which, 0, keepdims=False).astype(BF16)
        got = swap_bit(send, bit, size)
        block = lax.dynamic_index_in_dim(split, which, 0, keepdims=False) + got.astype(F32)
    return block[0]


def adam_step(weight_now, gradient, moments):
    first_moment = BETA_ONE * moments[0] + (1.0 - BETA_ONE) * gradient
    second_moment = BETA_TWO * moments[1] + (1.0 - BETA_TWO) * gradient * gradient
    first_fix = first_moment / (1.0 - BETA_ONE**ADAM_STEP)
    second_fix = second_moment / (1.0 - BETA_TWO**ADAM_STEP)
    change = -LEARN_RATE * (
        first_fix / (jnp.sqrt(second_fix) + ADAM_EPS) + DECAY_RATE * weight_now.astype(F32)
    )
    return (jnp.stack([first_moment, second_moment]), change)


def per_device(
    size,
    images,
    cotangent,
    image_count,
    w_qkv,
    w_out,
    w_up,
    w_down,
    vectors,
    head_bias,
    up_bias,
    *moment_list,
):
    core = lax.axis_index("tp")
    core_arr = core.reshape(1).astype(jnp.int32)
    rows = w_qkv.shape[1]
    heads_here = head_bias.shape[2]
    groups_here = up_bias.shape[1]
    cols = w_qkv.shape[3]
    dv, dh, du = vectors.shape[2], head_bias.shape[3], up_bias.shape[2]
    n_vec, n_hb, n_ub = vectors.size, head_bias.size, up_bias.size

    def pack(vec, hb, ub):
        lead = vec.shape[: vec.ndim - 3]
        flat = jnp.concatenate(
            [vec.reshape(lead + (-1,)), hb.reshape(lead + (-1,)), ub.reshape(lead + (-1,))], axis=-1
        )
        extra = rows * 128 - flat.shape[-1]
        flat = jnp.pad(flat, ((0, 0),) * len(lead) + ((0, extra),))
        return flat.reshape(lead + (rows, 128))

    def unpack(packed):
        lead = packed.shape[:-2]
        flat = packed.reshape(lead + (-1,))
        vec = flat[..., :n_vec].reshape(lead + vectors.shape)
        hb = flat[..., n_vec : n_vec + n_hb].reshape(lead + head_bias.shape)
        ub = flat[..., n_vec + n_hb : n_vec + n_hb + n_ub].reshape(lead + up_bias.shape)
        return vec, hb, ub

    def attn_shard(l):
        return jnp.concatenate([w_qkv[l].reshape(rows, 3 * cols), w_out[l].T], axis=1)

    def mlp_shard(l):
        return jnp.concatenate([w_up[l], w_down[l].T], axis=1)

    first = jnp.concatenate([attn_shard(0), pack(vectors, head_bias, up_bias)], axis=1)
    first = gather_rows(first, size)
    first_two = swap_cores(first)
    attn = [None, None]
    attn[0] = tuple(v[..., :HALF].reshape(D, HALF) for v in (first, first_two))
    small_own, small_oth = (unpack(v[..., HALF:]) for v in (first, first_two))
    vec_full = jnp.moveaxis(small_own[0], 0, 2).reshape(LAYERS, 6, D).astype(F32)
    hb_full = jnp.concatenate(
        [jnp.moveaxis(s[1], 0, 3).reshape(LAYERS, 2, -1) for s in (small_own, small_oth)], axis=2
    ).astype(F32)
    ub_full = jnp.concatenate(
        [jnp.moveaxis(s[2], 0, 2).reshape(LAYERS, 1, -1) for s in (small_own, small_oth)], axis=2
    ).astype(F32)
    small = jnp.concatenate([vec_full, hb_full], axis=1)

    def mlp_parts(block):
        return block[..., :HALF].reshape(D, HALF), block[..., HALF:].reshape(D, HALF)

    mlp = gather_rows(mlp_shard(0), size)
    mlp_two = swap_cores(mlp)
    ups0, downs0 = zip(mlp_parts(mlp), mlp_parts(mlp_two))

    last = gather_rows(jnp.concatenate([attn_shard(1), mlp_shard(1)], axis=1), size)
    last_two = swap_cores(last)
    attn1 = tuple(v[..., :HALF].reshape(D, HALF) for v in (last, last_two))
    ups1, downs1 = zip(mlp_parts(last[..., HALF:]), mlp_parts(last_two[..., HALF:]))

    mid0, qkv0, probs0, att0 = run_attn0(core_arr, images, *attn[0], small[0])
    x1, z0, gp0 = run_mlp0(mid0, ups0, downs0, small[0], ub_full[0])
    count = lax.dynamic_slice_in_dim(image_count[0], core, 1)
    (acts, g0, ga_own, ga_oth, gu_own, gu_oth, gd_own, gd_oth, gs1, gub1) = run_layer1(
        core_arr, count, x1, cotangent, attn1, ups1, downs1, small[1], ub_full[1]
    )

    def reduce_group(own, oth):
        own = jnp.concatenate(own, axis=1)
        oth = jnp.concatenate(oth, axis=1)
        total = own.astype(F32) + swap_cores(oth).astype(F32)
        return scatter_rows(total.reshape(size, rows, -1), size)

    sum1 = reduce_group((ga_own, gu_own, gd_own), (ga_oth, gu_oth, gd_oth))
    dm0, gu_own, gu_oth, gd_own, gd_oth, gs0m, gub0 = run_mlp0_back(
        g0, mid0, z0, gp0, ups0, downs0, small[0]
    )
    sum0m = reduce_group((gu_own, gd_own), (gu_oth, gd_oth))
    dx, ga_own, ga_oth, gs0a = run_attn0_back(
        core_arr, images, dm0, qkv0, probs0, att0, *attn[0], small[0]
    )
    g_small = jnp.stack([gs0m + gs0a, gs1])
    g_ub = jnp.stack([gub0, gub1])

    def small_pack(h):
        c = slice(h * cols, (h + 1) * cols)
        f = slice(h * (FF // 2), (h + 1) * (FF // 2))
        vec = jnp.moveaxis(g_small[:, :6].reshape(LAYERS, 6, size, dv), 2, 0)
        hb = jnp.moveaxis(g_small[:, 6:8, c].reshape(LAYERS, 2, heads_here, size, dh), 3, 0)
        ub = jnp.moveaxis(g_ub[:, 0, f].reshape(LAYERS, groups_here, size, du), 2, 0)
        return pack(vec, hb, ub).reshape(D, 128).astype(BF16)

    sum0a = reduce_group((ga_own, small_pack(0)), (ga_oth, small_pack(1)))
    g_vec, g_hb, g_ub_own = unpack(sum0a[:, HALF:])
    attn_sums = (sum0a[:, :HALF], sum1[:, :HALF])
    mlp_sums = (sum0m, sum1[:, HALF:])
    owned = (
        jnp.stack([v[:, : 3 * cols].reshape(rows, 3, cols) for v in attn_sums]),
        jnp.stack([v[:, 3 * cols :].T for v in attn_sums]),
        jnp.stack([v[:, :HALF] for v in mlp_sums]),
        jnp.stack([v[:, HALF:].T for v in mlp_sums]),
        g_vec,
        g_hb,
        g_ub_own,
    )

    def both(own):
        other = swap_cores(own)
        low = core == 0
        return jnp.concatenate([jnp.where(low, own, other), jnp.where(low, other, own)])

    out_acts = both(acts)
    input_grad = both(dx)
    param_list = (w_qkv, w_out, w_up, w_down, vectors, head_bias, up_bias)
    new_moments = []
    updates = []
    for index_p in range(7):
        moved, change = adam_step(param_list[index_p], owned[index_p], moment_list[index_p])
        new_moments.append(moved)
        updates.append(change)
    return (out_acts, input_grad, *owned, *new_moments, *updates)


def solution(mesh):
    placed = (
        P("fsdp", None, None),
        P("fsdp", None, None),
        P("fsdp", None),
        P(None, "fsdp", None, "tp"),
        P(None, "tp", "fsdp"),
        P(None, "fsdp", "tp"),
        P(None, "tp", "fsdp"),
        P(None, None, "fsdp"),
        P(None, None, "tp", "fsdp"),
        P(None, "tp", "fsdp"),
        P(None, None, "fsdp", None, "tp"),
        P(None, None, "tp", "fsdp"),
        P(None, None, "fsdp", "tp"),
        P(None, None, "tp", "fsdp"),
        P(None, None, None, "fsdp"),
        P(None, None, None, "tp", "fsdp"),
        P(None, None, "tp", "fsdp"),
    )
    return jax.shard_map(
        partial(per_device, mesh.shape["fsdp"]),
        mesh=mesh,
        in_specs=placed,
        out_specs=(
            P("fsdp", None, None),
            P("fsdp", None, None),
            P(None, "fsdp", None, "tp"),
            P(None, "tp", "fsdp"),
            P(None, "fsdp", "tp"),
            P(None, "tp", "fsdp"),
            P(None, None, "fsdp"),
            P(None, None, "tp", "fsdp"),
            P(None, "tp", "fsdp"),
            P(None, None, "fsdp", None, "tp"),
            P(None, None, "tp", "fsdp"),
            P(None, None, "fsdp", "tp"),
            P(None, None, "tp", "fsdp"),
            P(None, None, None, "fsdp"),
            P(None, None, None, "tp", "fsdp"),
            P(None, None, "tp", "fsdp"),
            P(None, "fsdp", None, "tp"),
            P(None, "tp", "fsdp"),
            P(None, "fsdp", "tp"),
            P(None, "tp", "fsdp"),
            P(None, None, "fsdp"),
            P(None, None, "tp", "fsdp"),
            P(None, "tp", "fsdp"),
        ),
        check_vma=False,
    )
```
